256 devices in a mesh: view: 16 (over z, x_hi), row: 4 (over x_lo, core), col: 4 (over y).
Axes of the slice: x: 4 (x_hi: 2, x_lo: 2; x = x_hi * 2 + x_lo), y: 4, z: 8, core: 2. Of those that a mesh axis runs over, the one named last changes fastest.
Arguments:
- residual: bfloat16 [16, 32, 128, 1024], P('view', 'row', 'col'), may hold values from -6 to 6
- window_query: bfloat16 [16, 32, 128, 1024], P('view', 'row', 'col'), may hold values from -56 to 56
- window_pairs: bfloat16 [2, 16, 32, 128, 1024], P(None, 'view', 'row', 'col'), may hold values from -4 to 4
- near_output: bfloat16 [1024, 1024], P('view'), may hold values from -0.1875 to 0.1875
- norm_gain: float32 [1024], replicated, may hold values from 0.1 to 1.9
- cross_input: bfloat16 [1024, 3072], P('view'), may hold values from -0.125 to 0.125
- head_gain: float32 [2, 64], replicated, may hold values from 0.7 to 6
- cross_output: bfloat16 [1024, 1024], P('view'), may hold values from -0.1875 to 0.1875
Outputs:
- block_out: bfloat16 [16, 32, 128, 1024], P('view', 'row', 'col')
The draws below stay inside these ranges and needn't reach their ends.
All inputs are finite; a program needn't handle non-finite values.
Results may differ from the reference program's by a relative error of at most 0.018.
Values may be sent and summed in bfloat16 or wider, within the bound.
A program may use at most 128 MiB of HBM per device.

```python
import math
import jax
import jax.numpy as jnp
from jax import lax

D = 1024
HEAD_DIM = 64
WINDOW = 13
RADIUS = 6
TILE_ROWS = 8
TILE_COLS = 32
VIEWS = 16
ROWS = 32
COLS = 128


def attention_inputs(key):
    shape = (3, VIEWS, ROWS, COLS, D)
    values = jax.random.truncated_normal(jax.random.fold_in(key, 11), -4.0, 4.0, shape, jnp.float32)
    return values


def draw_window_query(key, part):
    return attention_inputs(key)[0].astype(jnp.bfloat16)


def draw_window_pairs(key, part):
    return attention_inputs(key)[1:].astype(jnp.bfloat16)


def draw_cross_input(key, part):
    scale = D ** (-0.5)
    weight = jax.random.truncated_normal(key, -4.0, 4.0, (D, 3 * D), jnp.float32) * scale
    return weight.astype(jnp.bfloat16)


def draw_head_gain(key, part):
    gain_vec = jnp.exp(jax.random.uniform(key, (2, HEAD_DIM), jnp.float32, math.log(0.7), math.log(1.8)))
    return gain_vec


def steps_of(key, dims, split, low, top_value):
    level = 1.0
    for axis_at, parts in split:
        heights = jax.random.uniform(jax.random.fold_in(jax.random.fold_in(key, 6), axis_at), (parts,), jnp.float32, low / len(split), top_value / len(split))
        level = level * jnp.repeat(jnp.exp(heights), dims[axis_at] // parts).reshape((-1,) + (1,) * (len(dims) - 1 - axis_at))
    return level


def scatter_about(own_key, extent, deviation, reach, cuts=(), kind=jnp.bfloat16):
    loudness = steps_of(own_key, extent, cuts, -0.22, 0.18) if cuts else 1.0
    entries = jax.random.normal(own_key, extent, jnp.float32) * deviation * loudness
    return jnp.minimum(jnp.maximum(entries, -reach), reach).astype(kind)


def setup_inputs(seed: int = 0) -> dict:
    key_list = jax.random.split(jax.random.key(seed), 9)
    residual = scatter_about(key_list[0], (VIEWS, ROWS, COLS, D), 1.0, 6.0, ((0, 16), (1, 4), (2, 4)))
    window_query = draw_window_query(jax.random.fold_in(key_list[8], 71), 0)
    window_pairs = draw_window_pairs(jax.random.fold_in(key_list[8], 71), 0)
    near_output = scatter_about(key_list[3], (D, D), D ** -0.5, 0.1875, ((0, 16),))
    norm_gain = jnp.clip(1.0 + 0.18 * jax.random.normal(key_list[4], (D,), jnp.float32), 0.1, 1.9)
    cross_input = draw_cross_input(jax.random.fold_in(key_list[8], 71), 0)
    head_gain = draw_head_gain(jax.random.fold_in(key_list[8], 71), 0)
    cross_output = scatter_about(key_list[7], (D, D), D ** -0.5, 0.1875, ((0, 16),))
    return dict(residual=residual, window_query=window_query, window_pairs=window_pairs, near_output=near_output, norm_gain=norm_gain, cross_input=cross_input, head_gain=head_gain, cross_output=cross_output)


def window_mask(span_count, offset, total):
    queried = offset + jnp.arange(span_count, dtype=jnp.int32)
    keyed = offset - RADIUS + jnp.arange(span_count + 2 * RADIUS, dtype=jnp.int32)
    first_at = jnp.clip(queried - RADIUS, 0, total - WINDOW)
    return (keyed[None, :] >= first_at[:, None]) & (keyed[None, :] <= first_at[:, None] + WINDOW - 1)

def both_masks(tile_rows, tile_cols, row_start, col_start, row_count, col_count):
    by_row = window_mask(tile_rows, row_start, row_count)
    by_col = window_mask(tile_cols, col_start, col_count)
    joined = by_row[:, None, :, None] & by_col[None, :, None, :]
    return joined.reshape(tile_rows * tile_cols, (tile_rows + 2 * RADIUS) * (tile_cols + 2 * RADIUS))

def neighborhood(queries, key_tile, value_tile, allowed):
    token_count = queries.shape[0] * queries.shape[1]
    span_total = key_tile.shape[0] * key_tile.shape[1]
    features = queries.shape[2]
    head_count = features // HEAD_DIM
    query_heads = queries.reshape(token_count, head_count, HEAD_DIM).transpose(1, 0, 2)
    key_heads = key_tile.reshape(span_total, head_count, HEAD_DIM).transpose(1, 0, 2)
    value_heads = value_tile.reshape(span_total, head_count, HEAD_DIM).transpose(1, 0, 2)

    def one_head(pieces):
        query_h, key_h, value_h = pieces
        scores = jnp.dot(query_h, key_h.T, preferred_element_type=jnp.float32) * HEAD_DIM ** (-0.5)
        scores = jnp.where(allowed, scores, -jnp.inf)
        highest = lax.optimization_barrier(jnp.max(scores, axis=1, keepdims=True))
        exponent = jnp.exp(scores - highest)
        summed = lax.optimization_barrier(jnp.sum(exponent, axis=1, keepdims=True))
        mixture = jnp.dot(exponent.astype(jnp.bfloat16), value_h, preferred_element_type=jnp.float32)
        return (mixture / summed).astype(jnp.bfloat16)
    result = lax.map(one_head, (query_heads, key_heads, value_heads))
    return result.transpose(1, 0, 2).reshape(token_count, features)

def rms_scale(values, gain_vec, epsilon):
    meansq = lax.optimization_barrier(jnp.mean(values * values, axis=-1, keepdims=True))
    return values * lax.rsqrt(meansq + epsilon) * gain_vec

def split_projected(projected, head_gain, features):
    token_count = projected.shape[0]
    head_count = features // HEAD_DIM
    queried = rms_scale(projected[:, :features].reshape(token_count, head_count, HEAD_DIM), head_gain[0], 1e-06)
    keyed = rms_scale(projected[:, features:2 * features].reshape(token_count, head_count, HEAD_DIM), head_gain[1], 1e-06)
    return (queried.astype(jnp.bfloat16).reshape(token_count, features), keyed.astype(jnp.bfloat16).reshape(token_count, features), projected[:, 2 * features:].astype(jnp.bfloat16))

def across(queries, key_views, value_views):
    view_count, token_count, features = queries.shape
    other_count = key_views.shape[0]
    head_count = features // HEAD_DIM
    queried = queries.astype(jnp.float32).reshape(view_count, token_count, head_count, HEAD_DIM)
    keyed = key_views.astype(jnp.float32).reshape(other_count, token_count, head_count, HEAD_DIM)
    valued = value_views.astype(jnp.float32).reshape(other_count, token_count, head_count, HEAD_DIM)
    scores = jnp.einsum('vnhd,wnhd->nhvw', queried, keyed) * HEAD_DIM ** (-0.5)
    highest = lax.optimization_barrier(jnp.max(scores, axis=3, keepdims=True))
    exponent = jnp.exp(scores - highest)
    summed = lax.optimization_barrier(jnp.sum(exponent, axis=3))
    rounded = lax.optimization_barrier(exponent.astype(jnp.bfloat16)).astype(jnp.float32)
    mixture = jnp.einsum('nhvw,wnhd->vnhd', rounded, valued)
    mixture = mixture / jnp.transpose(summed, (2, 0, 1))[..., None]
    return mixture.astype(jnp.bfloat16).reshape(view_count, token_count, features)

def reference(residual, window_query, window_pairs, near_output, norm_gain, cross_input, head_gain, cross_output):
    view_count, row_count, col_count, features = residual.shape
    tile_size = TILE_ROWS * TILE_COLS
    tiles_down = row_count // TILE_ROWS
    tiles_across = col_count // TILE_COLS
    padded = jnp.pad(window_pairs, ((0, 0), (0, 0), (RADIUS, RADIUS), (RADIUS, RADIUS), (0, 0)))

    def one_tile(tile_index):
        view_index = tile_index // (tiles_down * tiles_across)
        within = tile_index % (tiles_down * tiles_across)
        row_start = (within // tiles_across * TILE_ROWS).astype(jnp.int32)
        col_start = (within % tiles_across * TILE_COLS).astype(jnp.int32)
        anchor = jnp.zeros((), jnp.int32)
        queries = lax.dynamic_slice(window_query, (view_index, row_start, col_start, anchor), (1, TILE_ROWS, TILE_COLS, features))[0]
        nearby = lax.dynamic_slice(padded, (anchor, view_index, row_start, col_start, anchor), (2, 1, TILE_ROWS + 2 * RADIUS, TILE_COLS + 2 * RADIUS, features))
        allowed = both_masks(TILE_ROWS, TILE_COLS, row_start, col_start, row_count, col_count)
        return neighborhood(queries, nearby[0, 0], nearby[1, 0], allowed)
    attended = lax.map(one_tile, jnp.arange(view_count * tiles_down * tiles_across, dtype=jnp.int32))
    attended = attended.reshape(view_count, tiles_down, tiles_across, TILE_ROWS, TILE_COLS, features)
    attended = attended.transpose(0, 1, 3, 2, 4, 5).reshape(view_count, row_count * col_count, features)
    flat_res = residual.reshape(view_count, row_count * col_count, features)

    def project_view(pieces):
        residue, nearby = pieces
        hidden = (residue.astype(jnp.float32) + jnp.dot(nearby, near_output, preferred_element_type=jnp.float32)).astype(jnp.bfloat16)
        normed = rms_scale(hidden.astype(jnp.float32), norm_gain, 1e-05).astype(jnp.bfloat16)
        projected = jnp.dot(normed, cross_input, preferred_element_type=jnp.float32)
        return (hidden,) + split_projected(projected, head_gain, features)
    hidden, queried, keyed, valued = lax.map(project_view, (flat_res, attended))
    block_count = row_count * col_count // tile_size

    def regroup(values_in):
        return values_in.reshape(view_count, block_count, tile_size, features).transpose(1, 0, 2, 3)

    def cross_block(pieces):
        return across(pieces[0], pieces[1], pieces[2])
    crossed = lax.map(cross_block, (regroup(queried), regroup(keyed), regroup(valued)))
    crossed = crossed.transpose(1, 0, 2, 3).reshape(view_count, row_count * col_count, features)

    def finish(pieces):
        residue, mixture = pieces
        return (residue.astype(jnp.float32) + jnp.dot(mixture, cross_output, preferred_element_type=jnp.float32)).astype(jnp.bfloat16)
    block_out = lax.map(finish, (hidden, crossed))
    return block_out.reshape(view_count, row_count, col_count, features)
```

```python
import functools

import jax
import jax.numpy as jnp
from jax import lax
from jax.experimental import pallas as pl
from jax.experimental.pallas import tpu as pltpu
from jax.sharding import PartitionSpec as P

HEAD_DIM = 64
WINDOW = 13
RADIUS = 6
SIDE = 8
PAIR = 2 * HEAD_DIM
BIG = -1e9
F32 = jnp.float32
BF16 = jnp.bfloat16


def iota(shape, dim):
    return lax.broadcasted_iota(jnp.int32, shape, dim)


def attend(query, query_tags, key, key_tags, value):
    count = query.shape[0]
    low = (iota((1, PAIR), 1) < HEAD_DIM).astype(F32)
    query = query * BF16(HEAD_DIM**-0.5)
    first = query * low.astype(BF16)
    second = query * (1.0 - low).astype(BF16)
    left = jnp.concatenate(
        [
            jnp.concatenate([first, query_tags], axis=1),
            jnp.concatenate([second, query_tags], axis=1),
        ],
        axis=0,
    )
    right = jnp.concatenate([key, key_tags], axis=1)
    scores = lax.dot_general(left, right, (((1,), (1,)), ((), ())), preferred_element_type=F32)
    highest = jnp.max(scores, axis=1, keepdims=True)
    probs = jnp.exp(scores - highest).astype(BF16)
    mixed = jnp.concatenate([value, jnp.ones(value.shape, BF16)], axis=1)
    out = jnp.dot(probs, mixed, preferred_element_type=F32)
    pick = iota((count, PAIR), 1) < HEAD_DIM
    top = jnp.where(pick, out[:count, :PAIR], out[count:, :PAIR])
    below = jnp.where(pick, out[:count, PAIR:], out[count:, PAIR:])
    return top / below


def window_ok(queried, keyed, total):
    first_at = jnp.clip(queried - RADIUS, 0, total - WINDOW)
    return (keyed >= first_at) & (keyed <= first_at + WINDOW - 1)


def near_start(half, row_start, part_rows, span_rows, rows_total, held_rows):
    at = row_start + half * part_rows
    first = jnp.clip(at - RADIUS, 0, rows_total - WINDOW) - (row_start - RADIUS)
    return jnp.minimum(first, held_rows - span_rows)


def near_key_tags(half, start, row_start, col_start, part_rows, shape, rows_total, cols_total):
    lane = iota(shape, 2)
    key_row = row_start - RADIUS + start + iota(shape, 0)
    key_col = col_start - SIDE + iota(shape, 1)
    row_ok = window_ok(row_start + half * part_rows + lane, key_row, rows_total)
    col_ok = window_ok(col_start + lane - 32, key_col, cols_total)
    bad = ((lane < part_rows) & ~row_ok) | ((lane >= 32) & (lane < 64) & ~col_ok)
    return jnp.where(bad, BIG, 0.0).astype(BF16).reshape(shape[0] * shape[1], shape[2])


def near_query_tags(part_rows, cols):
    shape = (part_rows, cols, PAIR)
    lane = iota(shape, 2)
    hit = (lane == iota(shape, 0)) | (lane == 32 + iota(shape, 1))
    return jnp.where(hit, 1.0, 0.0).astype(BF16).reshape(part_rows * cols, PAIR)


def head_norm(values, gain_row, ones_block):
    squares = values * values
    upper = squares.astype(BF16)
    lower = (squares - upper.astype(F32)).astype(BF16)
    total = jnp.dot(
        jnp.concatenate([upper, lower], axis=1), ones_block, preferred_element_type=F32
    )
    return (values * lax.rsqrt(total * (1.0 / HEAD_DIM) + 1e-06) * gain_row).astype(BF16)


def near_kernel(rows_total, cols_total, query, pairs, out, key_tags):
    rows, cols, features = query.shape
    held_rows, held_cols = pairs.shape[1], pairs.shape[2]
    part_rows = rows // 2
    span_rows = part_rows + 2 * RADIUS
    row_start = lax.axis_index("row") * rows
    col_start = lax.axis_index("col") * cols
    query_tags = near_query_tags(part_rows, cols)
    part = part_rows * cols
    for half in range(2):
        start = near_start(half, row_start, part_rows, span_rows, rows_total, held_rows)
        key_tags[...] = near_key_tags(
            half, start, row_start, col_start, part_rows,
            (span_rows, held_cols, PAIR), rows_total, cols_total,
        )

        @pl.loop(0, features // PAIR)
        def _(at):
            lanes = pl.ds(pl.multiple_of(at * PAIR, PAIR), PAIR)
            queried = query[half * part_rows : (half + 1) * part_rows, :, lanes]
            key = pairs[0, pl.ds(start, span_rows), :, lanes].reshape(span_rows * held_cols, PAIR)
            value = pairs[1, pl.ds(start, span_rows), :, lanes].reshape(span_rows * held_cols, PAIR)
            result = attend(
                queried.reshape(part, PAIR), query_tags, key, key_tags[...], value
            )
            out[half * part : (half + 1) * part, lanes] = result.astype(BF16)


def cross_kernel(views, hidden, gain, weight, head_gain, last, out, normed, mixed):
    tokens, features = hidden.shape
    pixels = tokens // views
    x = hidden[...].astype(F32)
    meansq = jnp.mean(x * x, axis=1, keepdims=True)
    normed[...] = (x * lax.rsqrt(meansq + 1e-05) * gain[...]).astype(BF16)
    shape = (views, pixels, PAIR)
    same = (iota(shape, 2) == iota(shape, 1)).reshape(tokens, PAIR)
    tagged = iota(shape, 2).reshape(tokens, PAIR) < pixels
    query_tags = jnp.where(same, 1.0, 0.0).astype(BF16)
    key_tags = jnp.where(tagged & ~same, BIG, 0.0).astype(BF16)
    block = jnp.where(
        (iota((PAIR, PAIR), 0) < HEAD_DIM) == (iota((PAIR, PAIR), 1) < HEAD_DIM), 1.0, 0.0
    ).astype(BF16)
    ones_block = jnp.concatenate([block, block], axis=0)
    query_gain = jnp.concatenate([head_gain[0:1, :]] * 2, axis=1)
    key_gain = jnp.concatenate([head_gain[1:2, :]] * 2, axis=1)
    wide = 2 * PAIR

    @pl.loop(0, features // wide)
    def _(at):
        base = pl.multiple_of(at * wide, wide)
        q4, k4, v4 = (
            jnp.dot(
                normed[...], weight[:, pl.ds(part * features + base, wide)],
                preferred_element_type=F32,
            )
            for part in range(3)
        )
        for piece in range(2):
            cut = slice(piece * PAIR, (piece + 1) * PAIR)
            result = attend(
                head_norm(q4[:, cut], query_gain, ones_block), query_tags,
                head_norm(k4[:, cut], key_gain, ones_block), key_tags,
                v4[:, cut].astype(BF16),
            )
            mixed[:, pl.ds(base + piece * PAIR, PAIR)] = result.astype(BF16)

    @pl.loop(0, features // wide)
    def _(at):
        lanes = pl.ds(pl.multiple_of(at * wide, wide), wide)
        term = jnp.dot(mixed[...], last[:, lanes], preferred_element_type=F32)
        out[:, lanes] = (hidden[:, lanes].astype(F32) + term).astype(BF16)


def padded(block, sides):
    for axis, dim, width in sides:
        count = lax.axis_size(axis)
        forward = [(i, i + 1) for i in range(count - 1)]
        backward = [(target, source) for source, target in forward]
        low = lax.ppermute(
            lax.slice_in_dim(block, block.shape[dim] - width, None, axis=dim), axis, forward
        )
        high = lax.ppermute(lax.slice_in_dim(block, 0, width, axis=dim), axis, backward)
        block = jnp.concatenate([low, block, high], axis=dim)
    return block


def local(residual, window_query, window_pairs, near_output, norm_gain, cross_input, head_gain, cross_output):
    _, rows, cols, features = residual.shape
    tokens = rows * cols
    views = lax.axis_size("view")
    rows_total = rows * lax.axis_size("row")
    cols_total = cols * lax.axis_size("col")
    near_weight = lax.all_gather(near_output, "view", axis=0, tiled=True)
    in_weight = lax.all_gather(cross_input, "view", axis=0, tiled=True)
    out_weight = lax.all_gather(cross_output, "view", axis=0, tiled=True)
    nearby = padded(window_pairs[:, 0], (("row", 1, RADIUS), ("col", 2, SIDE)))
    span = (rows // 2 + 2 * RADIUS) * nearby.shape[2]
    attended = pl.pallas_call(
        functools.partial(near_kernel, rows_total, cols_total),
        out_shape=jax.ShapeDtypeStruct((tokens, features), BF16),
        in_specs=[pl.BlockSpec(memory_space=pltpu.VMEM)] * 2,
        out_specs=pl.BlockSpec(memory_space=pltpu.VMEM),
        scratch_shapes=[pltpu.VMEM((span, PAIR), BF16)],
        compiler_params=pltpu.CompilerParams(vmem_limit_bytes=48 << 20),
        name="near_attention",
    )(window_query[0], nearby)
    near_term = jnp.dot(attended, near_weight, preferred_element_type=F32)
    hidden = (residual[0].reshape(tokens, features).astype(F32) + near_term).astype(BF16)
    moved = lax.all_to_all(
        hidden.reshape(views, tokens // views, features), "view", split_axis=0, concat_axis=0, tiled=True
    ).reshape(tokens, features)
    done = pl.pallas_call(
        functools.partial(cross_kernel, views),
        out_shape=jax.ShapeDtypeStruct((tokens, features), BF16),
        in_specs=[pl.BlockSpec(memory_space=pltpu.VMEM)] * 5,
        out_specs=pl.BlockSpec(memory_space=pltpu.VMEM),
        scratch_shapes=[pltpu.VMEM((tokens, features), BF16)] * 2,
        compiler_params=pltpu.CompilerParams(vmem_limit_bytes=48 << 20),
        name="cross_attention",
    )(moved, norm_gain.reshape(1, features), in_weight, head_gain, out_weight)
    back = lax.all_to_all(
        done.reshape(views, tokens // views, features), "view", split_axis=0, concat_axis=0, tiled=True
    )
    return back.reshape(1, rows, cols, features)


def solution(mesh):
    in_specs = (
        P("view", "row", "col", None),
        P("view", "row", "col", None),
        P(None, "view", "row", "col", None),
        P("view", None),
        P(),
        P("view", None),
        P(),
        P("view", None),
    )
    out_specs = P("view", "row", "col", None)
    return jax.shard_map(local, mesh=mesh, in_specs=in_specs, out_specs=out_specs, check_vma=False)
```
